512 devices in a mesh: grp: 8 (over y, core), dev: 64 (over x, z).
Axes of the slice: x: 4, y: 4, z: 16, core: 2. Of those that a mesh axis runs over, the one named last changes fastest.
Arguments:
- offsets: float32 [2048, 3, 512], P(('grp', 'dev')), may hold values from 0 to 1
- sketch: bfloat16 [2048, 512, 256], P(('grp', 'dev')), may hold values from -6 to 6
- pattern: int32 [2048, 6], P(('grp', 'dev')), may hold values 0 or 1
- point_order: int32 [2048, 512], P(('grp', 'dev')), may hold values from 0 to 511, each once within a row
Outputs:
- basis: bfloat16 [2048, 512, 256], P(('grp', 'dev'))
- basis_factor: float32 [2048, 256, 256], P(('grp', 'dev'))
The draws below stay inside these ranges and needn't reach their ends.
Inputs may be any that keep to these rules, and one draw needn't show every extreme that they name: `point_order`: each row is a permutation of 0 .. 511.
All inputs are finite; a program needn't handle non-finite values. No bound on the sum of `pattern` on one device may be relied on, other than what follows from the above.
Results may differ from the reference program's by a relative error of at most 0.0082.
Values may be sent and summed in bfloat16 or wider, within the bound.
A program may use at most 64 MiB of HBM per device.

```python
import math
import jax
import jax.numpy as jnp
from jax import lax

M = 512
R = 256
W = 4
NADM = 6
NCL = 2048


def place_ends(entries, stream_key, smallest, high):
    longest = entries.shape.index(max(entries.shape))
    spots = []
    for shift in (0, 1):
        where = [jax.random.randint(jax.random.fold_in(stream_key, axis), (), 0, length) for axis, length in enumerate(entries.shape)]
        where[longest] = (where[longest] + shift) % entries.shape[longest]
        spots.append(tuple(where))
    return entries.at[spots[0]].set(smallest).at[spots[1]].set(high)


def level_of(own_key, extent, pieces, smallest, top_value):
    loudness, own = 1.0, jax.random.fold_in(own_key, 6)
    for position, blocks in pieces:
        draws = jnp.exp(jax.random.uniform(jax.random.fold_in(own, position), (blocks,), jnp.float32, smallest / len(pieces), top_value / len(pieces)))
        loudness = loudness * jnp.repeat(draws, extent[position] // blocks).reshape([-1 if axis == position else 1 for axis in range(len(extent))])
    return loudness


def gaussian(own_key, shape, scale, limit, cuts=(), kind=jnp.bfloat16):
    result = scale * jax.random.normal(own_key, shape, jnp.float32)
    if cuts:
        result = result * level_of(own_key, shape, cuts, -0.22, 0.18)
    return jnp.clip(result, -limit, limit).astype(kind)


def setup_inputs(seed: int = 0) -> dict:
    seeds = jax.random.split(jax.random.key(seed), 5)
    offsets = jnp.clip(1.0 * jax.random.uniform(seeds[0], (NCL, 3, M), jnp.float32) ** level_of(seeds[0], (NCL, 3, M), ((0, 512),), -0.2, 0.2), 0.0, 1.0)
    sketch = gaussian(seeds[1], (NCL, M, R), 1.0, 6.0, ((0, 512),))
    pattern = place_ends((jax.random.randint(seeds[2], (NCL, NADM), 0, 3) < 2).astype(jnp.int32), jax.random.fold_in(seeds[2], 1), 0, 1)
    point_order = jax.vmap(lambda own: jax.random.permutation(own, M))(jax.random.split(seeds[3], NCL)).reshape((NCL, M)).astype(jnp.int32)
    return dict(offsets=offsets, sketch=sketch, pattern=pattern, point_order=point_order)


wave_number = 40.0
decay_length = 4.0
softening = 0.5

def offset_table(reach):
    return [-value for value in range(reach, 1, -1)] + list(range(2, reach + 1))

def with_index(points, start):
    count = points.shape[0]
    index = (start + jnp.arange(count, dtype=jnp.int32)).astype(points.dtype)
    unit = jnp.zeros((1, 3, 1), points.dtype).at[0, 0, 0].set(1.0)
    return points + index[:, None, None] * unit

def kernel_block(target_side, source_side, weight):
    squared = (target_side[0][:, None] - source_side[0][None, :]) ** 2
    squared = squared + (target_side[1][:, None] - source_side[1][None, :]) ** 2
    squared = squared + (target_side[2][:, None] - source_side[2][None, :]) ** 2
    distance = jnp.sqrt(squared)
    values = jnp.cos(wave_number * distance) * jnp.exp(-distance / decay_length) / (distance + softening)
    scale = weight * (1.0 / math.sqrt(target_side.shape[1]))
    return (values * scale).astype(jnp.bfloat16)

def basis_of(samples):
    gram = jnp.dot(samples.T.astype(jnp.float32), samples.astype(jnp.float32), precision=lax.Precision.HIGHEST, preferred_element_type=jnp.float32)
    width = gram.shape[0]
    shift = 0.01 * jnp.trace(gram) / width + 1e-05
    lower = jnp.linalg.cholesky(gram + shift * jnp.eye(width, dtype=jnp.float32))
    rows = jax.scipy.linalg.solve_triangular(lower, samples.T, lower=True)
    return (rows.T.astype(jnp.bfloat16), lower.T)

def reference(offsets, sketch, pattern, point_order):
    total_clusters = offsets.shape[0]
    places = with_index(offsets, 0)
    order = jnp.broadcast_to(point_order[:, None, :], places.shape)
    targets = jnp.take_along_axis(places, order, axis=2)
    padded_offsets = jnp.pad(offsets, ((W, W), (0, 0), (0, 0)))
    window_places = with_index(padded_offsets, -W)
    window_sketch = jnp.pad(sketch, ((W, W), (0, 0), (0, 0)))
    table = offset_table(W)

    def one_cluster(cluster):
        target_side = lax.dynamic_index_in_dim(targets, cluster, 0, keepdims=False)
        total = jnp.zeros((sketch.shape[1], sketch.shape[2]), jnp.float32)
        for column, shift_value in enumerate(table):
            source = cluster + W + shift_value
            source_side = lax.dynamic_index_in_dim(window_places, source, 0, keepdims=False)
            source_rows = lax.dynamic_index_in_dim(window_sketch, source, 0, keepdims=False)
            weight = lax.dynamic_index_in_dim(pattern[:, column], cluster, 0, keepdims=False).astype(jnp.float32)
            block = kernel_block(target_side, source_side, weight)
            total = total + jnp.dot(block.astype(jnp.float32), source_rows.astype(jnp.float32), preferred_element_type=jnp.float32)
        return basis_of(total)
    basis, basis_factor = lax.map(one_cluster, jnp.arange(total_clusters, dtype=jnp.int32), batch_size=8)
    return (basis, basis_factor)
```

```python
import math, functools
import numpy as np
import jax, jax.numpy as jnp
from jax import lax
from jax.experimental import pallas as pl
from jax.experimental.pallas import tpu as pltpu
F32=jnp.float32; BF=jnp.bfloat16
M=512
def cos_coeffs(deg):
    n=4000
    t=np.cos((np.arange(n)+.5)*np.pi/n)
    z=0.125+0.125*t
    f=np.sqrt(z)
    c=np.polynomial.chebyshev.Chebyshev.fit(z,np.cos(2*np.pi*f),deg,domain=[0,0.25])
    p=c.convert(kind=np.polynomial.Polynomial,domain=[-1,1],window=[-1,1]).coef
    return [float(v) for v in p]
COS=cos_coeffs(5)
SCALE=1.0/math.sqrt(512)
def value(u):
    r=u*lax.rsqrt(u)
    y=r*(40.0/(2*math.pi))
    k=(y+12582912.0)-12582912.0
    f=y-k
    z=f*f
    p=COS[5]*SCALE
    for c in COS[4::-1]:
        p=p*z+c*SCALE
    h=jnp.exp2(r*(-0.25*math.log2(math.e))-jnp.log2(r+0.5))
    return p*h
def split3(x):
    h=x.astype(BF).astype(F32); m=(x-h).astype(BF).astype(F32); return h,m,x-h-m
def prep(off, c, t_ref, s_ref):
    ax=(off[0:1]+c)-c
    n=ax*ax
    rows=[ax]
    for d in (1,2):
        v=off[d:d+1]; rows.append(v); n=n+v*v
    one=jnp.ones_like(ax); zero=jnp.zeros_like(ax)
    for d,v in enumerate(rows):
        h,m,l=split3(v)
        if t_ref is not None:
            for q,w in enumerate((h,h,m,m,h,l)): t_ref[6*d+q:6*d+q+1,:]=w
        if s_ref is not None:
            for q,w in enumerate((h,m,h,m,l,h)): s_ref[6*d+q:6*d+q+1,:]=-2.0*w
        if d==0: hx=(h,m,l)
    n3=split3(n)
    for q in range(3):
        if t_ref is not None:
            t_ref[18+q:19+q,:]=n3[q]; t_ref[21+q:22+q,:]=one; t_ref[24+q:25+q,:]=hx[q]; t_ref[27+q:28+q,:]=zero
        if s_ref is not None:
            s_ref[18+q:19+q,:]=one; s_ref[21+q:22+q,:]=n3[q]; s_ref[24+q:25+q,:]=zero; s_ref[27+q:28+q,:]=hx[q]
    if t_ref is not None:
        t_ref[30:31,:]=one; t_ref[31:32,:]=zero
    if s_ref is not None:
        s_ref[30:31,:]=zero; s_ref[31:32,:]=zero
def t_of(t, o):
    row=lax.broadcasted_iota(jnp.int32,t.shape,0)
    return (t+jnp.where((row>=27)&(row<30),2.0*o,0.0)).astype(BF)
def s_of(s, o):
    row=lax.broadcasted_iota(jnp.int32,s.shape,0)
    return (s+jnp.where((row>=24)&(row<27),-2.0*o,0.0)+jnp.where(row==30,o*o,0.0)).astype(BF)
from jax.sharding import PartitionSpec as P
MESH_ID=pl.DeviceIdType.MESH
CW=256
L_ORDER=(2,3,1,0); R_ORDER=(1,0,2,3)
def k1(groups, devs, count, off_ref, sk_ref, pat_ref, out_ref, hoff, own, hsk, tp, sp, so, ro, ss, rsem, loc):
    d=lax.axis_index("grp")*devs+lax.axis_index("dev")
    total=groups*devs
    right=lax.rem(d+1,total); left=lax.rem(d+total-1,total)
    rid=(right//devs,lax.rem(right,devs)); lid=(left//devs,lax.rem(left,devs))
    barrier=pltpu.get_barrier_semaphore()
    for n in (lid,rid):
        pl.semaphore_signal(barrier,inc=1,device_id=n,device_id_type=MESH_ID)
    local=pltpu.make_async_copy(sk_ref,own,loc)
    local.start()
    pl.semaphore_wait(barrier,2)
    def coff(side):
        return pltpu.make_async_remote_copy(off_ref,hoff.at[side],so.at[side],ro.at[side],device_id=rid if side==0 else lid,device_id_type=MESH_ID)
    def csk(side,j):
        return pltpu.make_async_remote_copy(sk_ref.at[j],hsk.at[side,j],ss.at[side,j],rsem.at[side,j],device_id=rid if side==0 else lid,device_id_type=MESH_ID)
    for side in (0,1): coff(side).start()
    for a,b in zip(L_ORDER,R_ORDER):
        csk(0,a).start(); csk(1,b).start()
    first=d*4
    ff=first.astype(F32)
    for s in range(4,8):
        prep(off_ref[s-4], ff+(s-4.0), tp.at[s-4], sp.at[s])
    out_ref[...]=jnp.zeros_like(out_ref)
    local.wait()
    def source(s,get):
        j=s-4
        tg=[i for i in range(4) if 2<=abs(j-i)<=4]
        i0,cnt=tg[0],len(tg)
        def body(t,_):
            i=i0+t
            oi=j-i; o=oi.astype(F32)
            k=jnp.where(oi<0,oi+4,oi+1)
            g=first+j
            w=jnp.where((g>=0)&(g<count),pat_ref[i,k],0).astype(F32)
            T=t_of(tp[i],o)
            acc=None
            for c in range(M//CW):
                S=s_of(sp[s,:,c*CW:(c+1)*CW],o)
                u=dot(T,S,0,0)
                kb=value(u).astype(BF)
                pr=dot(kb,get(c))
                acc=pr if acc is None else acc+pr
            out_ref[i]=out_ref[i]+w*acc
            return 0
        lax.fori_loop(0,cnt,body,0)
    def dot(a,b,ca=1,cb=0):
        return lax.dot_general(a,b,(((ca,),(cb,)),((),())),preferred_element_type=F32)
    for s in range(4,8):
        source(s,lambda c: own[s-4,c*CW:(c+1)*CW,:])
    for side in (0,1): coff(side).wait_recv()
    for s in range(4):
        prep(hoff[0,s], ff+(s-4.0), None, sp.at[s])
        prep(hoff[1,s], ff+(s+4.0), None, sp.at[8+s])
    for a,b in zip(L_ORDER,R_ORDER):
        csk(0,a).wait_recv()
        source(a,lambda c: hsk[0,a,c*CW:(c+1)*CW,:])
        csk(1,b).wait_recv()
        source(8+b,lambda c: hsk[1,b,c*CW:(c+1)*CW,:])
    for side in (0,1):
        coff(side).wait_send()
        for j in range(4): csk(side,j).wait_send()
def call1(mesh,offsets,sketch,pattern,count):
    g,dv=mesh.shape["grp"],mesh.shape["dev"]
    V=pl.BlockSpec(memory_space=pltpu.VMEM)
    return pl.pallas_call(functools.partial(k1,g,dv,count),out_shape=jax.ShapeDtypeStruct((4,512,256),F32),
      in_specs=[V,pl.BlockSpec(memory_space=pl.ANY),pl.BlockSpec(memory_space=pltpu.SMEM)],out_specs=V,
      scratch_shapes=[pltpu.VMEM((2,4,3,512),F32),pltpu.VMEM((4,512,256),BF),pltpu.VMEM((2,4,512,256),BF),
        pltpu.VMEM((4,32,512),F32),pltpu.VMEM((12,32,512),F32),
        pltpu.SemaphoreType.DMA((2,)),pltpu.SemaphoreType.DMA((2,)),pltpu.SemaphoreType.DMA((2,4)),pltpu.SemaphoreType.DMA((2,4)),pltpu.SemaphoreType.DMA],
      compiler_params=pltpu.CompilerParams(vmem_limit_bytes=50<<20,collective_id=0,has_side_effects=True))(offsets,sketch,pattern)
def cat3(xh,xl): pass
def hl(x):
    h=x.astype(BF); return h,(x-h.astype(F32)).astype(BF)
def dot(a,b,ca=1,cb=0):
    return lax.dot_general(a,b,(((ca,),(cb,)),((),())),preferred_element_type=F32)
NB=64; R=256; NC=4
def k2(s_ref, ord_ref, basis_ref, fac_ref, aug, xh, xl, xs):
    lane=lax.broadcasted_iota(jnp.int32,(NB,128),1)
    row=lax.broadcasted_iota(jnp.int32,(NB,128),0)
    r2=lax.broadcasted_iota(jnp.int32,(R,R),0); c2=lax.broadcasted_iota(jnp.int32,(R,R),1)
    eye=r2==c2
    for c in range(NC):
        st=s_ref[c].T
        aug[c,:,R:]=st
        th,tl=hl(st)
        g=dot(th,th,1,1)+(dot(th,tl,1,1)+dot(tl,th,1,1))
        tr=jnp.sum(jnp.where(eye,g,0.0),keepdims=True)
        shift=tr*(0.01/R)+1e-5
        aug[c,:,:R]=g+jnp.where(eye,shift,0.0)
    for jb in range(4):
        lt,half=jb//2,jb%2
        r0=jb*NB; rs=slice(r0,r0+NB); t0=lt*128; tile=slice(t0,t0+128)
        K=r0
        inA=(lane>=64) if half else (lane<64)
        other=(lane==row) if half else (lane==row+64)
        Ms=[]; lh=[None]*NC; ll=[None]*NC
        for c in range(NC):
            D=aug[c,rs,tile]
            if jb:
                lh[c]=xh[c,0:K,tile].T[64*half:64*half+64]
                ll[c]=xl[c,0:K,tile].T[64*half:64*half+64]
                bh,bl=xh[c,0:K,tile],xl[c,0:K,tile]
                D=D-(dot(lh[c],bh)+(dot(lh[c],bl)+dot(ll[c],bh)))
                aug[c,rs,tile]=D
            Mx=jnp.where(inA,D,jnp.where(other,1.0,0.0))
            Ms.append([Mx[8*g:8*g+8] for g in range(8)])
        rest=slice(t0+128,768)
        if jb:
            for c in range(NC):
                bh,bl=xh[c,0:K,rest],xl[c,0:K,rest]
                aug[c,rs,rest]=aug[c,rs,rest]-(dot(lh[c],bh)+(dot(lh[c],bl)+dot(ll[c],bh)))
        for j in range(NB):
            pj=64*half+j; g0,sj=j//8,j%8
            for c in range(NC):
                m=Ms[c]
                cb=[None]*8
                for g in range(g0,8):
                    cb[g]=jnp.broadcast_to(m[g][:,pj:pj+1],(8,128))
                rw=jnp.broadcast_to(m[g0][sj:sj+1,:],(8,128))
                pb=jnp.broadcast_to(cb[g0][sj:sj+1,:],(8,128))
                s=lax.rsqrt(pb)
                sc=rw*s
                xs[c,j:j+1,:]=sc[0:1]
                if j<NB-1:
                    q=sc*s
                    for g in range((j+1)//8,8):
                        m[g]=m[g]-cb[g]*q
        for c in range(NC):
            X=xs[c]
            U=jnp.where(inA&((lane-64*half)>=row),X,0.0)
            Li=X[:, 0:64] if half else X[:, 64:128]
            Lh,Ll=hl(Li)
            cols=slice(t0 if half==0 else t0+128,768)
            rh,rl=hl(aug[c,rs,cols])
            P=dot(Lh,rh)+(dot(Lh,rl)+dot(Ll,rh))
            ph,pl_=hl(P)
            xh[c,rs,cols]=ph; xl[c,rs,cols]=pl_
            if half==0:
                fac_ref[c,rs,tile]=jnp.where(inA,U,P[:,0:128])
                if lt==0: fac_ref[c,rs,128:256]=P[:,128:256]
            else:
                fac_ref[c,rs,tile]=U
                if lt==0: fac_ref[c,rs,128:256]=P[:,0:128]
            if lt==1: fac_ref[c,rs,0:128]=jnp.zeros((NB,128),F32)
    of=ord_ref[...].astype(F32)
    oT=jnp.concatenate([of,of],axis=0).T
    lane5=lax.broadcasted_iota(jnp.int32,(512,512),1).astype(F32)
    for c in range(NC):
        P=jnp.where(oT[:,c:c+1]==lane5,1.0,0.0).astype(BF)
        basis_ref[c]=dot(P,xh[c,:,R:],1,1).astype(BF)
def call2(samples,order,interpret=False):
    return pl.pallas_call(k2,out_shape=[jax.ShapeDtypeStruct((4,512,256),BF),jax.ShapeDtypeStruct((4,256,256),F32)],
      in_specs=[pl.BlockSpec(memory_space=pltpu.VMEM)]*2,out_specs=[pl.BlockSpec(memory_space=pltpu.VMEM)]*2,
      scratch_shapes=[pltpu.VMEM((4,256,768),F32),pltpu.VMEM((4,256,768),BF),pltpu.VMEM((4,256,768),BF),pltpu.VMEM((4,64,128),F32)],
      compiler_params=pltpu.CompilerParams(vmem_limit_bytes=50<<20))(samples,order)
def solution(mesh):
    placed=(P(("grp","dev"),None,None),P(("grp","dev"),None,None),P(("grp","dev"),None),P(("grp","dev"),None))
    devices=mesh.shape["grp"]*mesh.shape["dev"]
    def body(offsets,sketch,pattern,point_order):
        samples=call1(mesh,offsets,sketch,pattern,offsets.shape[0]*devices)
        return tuple(call2(samples,point_order))
    return jax.shard_map(body,mesh=mesh,in_specs=placed,out_specs=(P(("grp","dev"),None,None),P(("grp","dev"),None,None)),check_vma=False)
```

```python
import math, functools
import numpy as np
import jax, jax.numpy as jnp
from jax import lax
from jax.experimental import pallas as pl
from jax.experimental.pallas import tpu as pltpu
F32=jnp.float32; BF=jnp.bfloat16
M=512
def cos_coeffs(deg):
    n=4000
    t=np.cos((np.arange(n)+.5)*np.pi/n)
    z=0.125+0.125*t
    f=np.sqrt(z)
    c=np.polynomial.chebyshev.Chebyshev.fit(z,np.cos(2*np.pi*f),deg,domain=[0,0.25])
    p=c.convert(kind=np.polynomial.Polynomial,domain=[-1,1],window=[-1,1]).coef
    return [float(v) for v in p]
def sin_coeffs(deg):
    n=4000
    t=np.cos((np.arange(n)+.5)*np.pi/n)
    z=1/32+1/32*t
    g=np.sqrt(z)
    y=-np.sin(2*np.pi*g)/g
    w=np.sqrt(g)
    V=np.vander(z*16,deg+1,increasing=True)
    for _ in range(40):
        c=np.linalg.lstsq(V*(w*g)[:,None],y*w*g,rcond=None)[0]
        e=np.abs((V@c-y)*g)
        w=w*np.sqrt(1e-3+e/e.max()); w=w/w.max()
    return [float(v*16.0**n) for n,v in enumerate(c)]
SIN=sin_coeffs(3)
SIGMA=40.0/(2*math.pi)
SCALE=1.0/math.sqrt(512)
def value(u):
    y=u*lax.rsqrt(u)
    g=jnp.abs(y-jnp.round(y))-0.25
    z=g*g
    a=SCALE*SIGMA
    p=SIN[-1]*a
    for c in SIN[-2::-1]:
        p=p*z+c*a
    h=jnp.exp2(y*(-0.25*math.log2(math.e)/SIGMA)-jnp.log2(y+0.5*SIGMA))
    return (p*g)*h
def split3(x):
    h=x.astype(BF).astype(F32); m=(x-h).astype(BF).astype(F32); return h,m,x-h-m
def prep(off, c, t_ref, s_ref):
    x=jnp.concatenate([(off[0:1]+c)-c,off[1:3]],axis=0)
    if t_ref is not None:
        a=x*SIGMA
        n=a[0:1]*a[0:1]+a[1:2]*a[1:2]+a[2:3]*a[2:3]
        h,m,l=split3(a)
        for d in range(3):
            for q,w in enumerate((h,h,m,m,h,l)): t_ref[6*d+q:6*d+q+1,:]=w[d:d+1]
        one=jnp.ones_like(n)
        for q,w in enumerate(split3(n)):
            t_ref[18+q:19+q,:]=w; t_ref[21+q:22+q,:]=one
        t_ref[24:32,:]=jnp.zeros((8,x.shape[1]),F32)
    s_ref[0:3,:]=x
def s_rows(x, o, s_ref):
    b=jnp.concatenate([x[0:1]+o,x[1:3]],axis=0)*SIGMA
    n=b[0:1]*b[0:1]+b[1:2]*b[1:2]+b[2:3]*b[2:3]
    h,m,l=[-2.0*w for w in split3(b)]
    for d in range(3):
        for q,w in enumerate((h,m,h,m,l,h)): s_ref[6*d+q:6*d+q+1,:]=w[d:d+1]
    one=jnp.ones_like(n)
    for q,w in enumerate(split3(n)):
        s_ref[18+q:19+q,:]=one; s_ref[21+q:22+q,:]=w
    s_ref[24:32,:]=jnp.zeros((8,x.shape[1]),F32)
from jax.sharding import PartitionSpec as P
MESH_ID=pl.DeviceIdType.MESH
CHR=128
L_ORDER=(2,3,1,0); R_ORDER=(1,0,2,3)
def pair_list():
    order=[4,5,6,7]
    for a,b in zip(L_ORDER,R_ORDER): order+=[a,8+b]
    return [(s,i) for s in order for i in range(4) if 2<=abs(s-4-i)<=4]
PAIRS=pair_list()
def lookup(t,table):
    v=jnp.int32(table[0])
    for n in range(1,len(table)):
        if table[n]!=table[n-1]: v=jnp.where(t>=n,table[n],v)
    return v
def dot(a,b,ca=1,cb=0):
    return lax.dot_general(a,b,(((ca,),(cb,)),((),())),preferred_element_type=F32)
def stages(sk, tp, sp, sr, pat_ref, out_ref, u_ref, k_ref, first, count, CHR):
    def decode(t):
        t=jnp.clip(t,0,len(PAIRS)-1)
        return lookup(t,[p[0] for p in PAIRS]),lookup(t,[p[1] for p in PAIRS])
    def loadA(t):
        s,i=decode(t)
        o=(s-4-i).astype(F32)
        s_rows(sp[s],o,sr)
        return tp[i],sr[...].astype(BF)
    def Aval(ops,r):
        T,S=ops
        return dot(T[:,r*CHR:(r+1)*CHR],S,0,0)
    def A(ops,r):
        T,S=ops
        u_ref[r*CHR:(r+1)*CHR,:]=dot(T[:,r*CHR:(r+1)*CHR],S,0,0)
    def B(r):
        k_ref[r*CHR:(r+1)*CHR,:]=value(u_ref[r*CHR:(r+1)*CHR,:]).astype(BF)
    def infoC(t):
        s,i=decode(t)
        oi=s-4-i
        k=jnp.where(oi<0,oi+4,oi+1)
        g=first+s-4
        w=jnp.where((g>=0)&(g<count)&(t>=0),pat_ref[i,k],0).astype(F32)
        return s,i,w
    def C(info,r):
        s,i,w=info
        rows=slice(r*CHR,(r+1)*CHR)
        out_ref[i,rows,:]=out_ref[i,rows,:]+w*dot(k_ref[rows,:],sk[s])
    return loadA,A,B,infoC,C
def k1(groups, devs, count, off_ref, sk_ref, pat_ref, out_ref, hoff, sk, tf, tp, sp, sr, u_ref, k_ref, so, ro, ss, rsem, loc):
    d=lax.axis_index("grp")*devs+lax.axis_index("dev")
    total=groups*devs
    right=lax.rem(d+1,total); left=lax.rem(d+total-1,total)
    rid=(right//devs,lax.rem(right,devs)); lid=(left//devs,lax.rem(left,devs))
    barrier=pltpu.get_barrier_semaphore()
    for n in (lid,rid):
        pl.semaphore_signal(barrier,inc=1,device_id=n,device_id_type=MESH_ID)
    local=pltpu.make_async_copy(sk_ref,sk.at[4:8],loc)
    local.start()
    first=d*4
    ff=first.astype(F32)
    for s in range(4,8):
        prep(off_ref[s-4], ff+(s-4.0), tf, sp.at[s])
        tp[s-4]=tf[...].astype(BF)
    out_ref[...]=jnp.zeros_like(out_ref)
    k_ref[...]=jnp.zeros_like(k_ref)
    pl.semaphore_wait(barrier,2)
    def coff(side):
        return pltpu.make_async_remote_copy(off_ref,hoff.at[side],so.at[side],ro.at[side],device_id=rid if side==0 else lid,device_id_type=MESH_ID)
    def csk(side,j):
        return pltpu.make_async_remote_copy(sk_ref.at[j],sk.at[8*side+j],ss.at[side,j],rsem.at[side,j],device_id=rid if side==0 else lid,device_id_type=MESH_ID)
    for side in (0,1): coff(side).start()
    for a,b in zip(L_ORDER,R_ORDER):
        csk(0,a).start(); csk(1,b).start()
    loadA,A,B,infoC,C=stages(sk,tp,sp,sr,pat_ref,out_ref,u_ref,k_ref,first,count,CHR)
    N=M//CHR
    ops=loadA(jnp.int32(0))
    for r in range(N): A(ops,r)
    local.wait()
    def body(t,_):
        ops=loadA(t+1); info=infoC(t-1)
        for r in range(N):
            C(info,r); B(r); A(ops,r)
        return 0
    NLOC=6
    lax.fori_loop(0,NLOC-1,body,0)
    for side in (0,1): coff(side).wait_recv()
    for s in range(4):
        prep(hoff[0,s], ff+(s-4.0), None, sp.at[s])
        prep(hoff[1,s], ff+(s+4.0), None, sp.at[8+s])
    srcs=[p[0] for p in PAIRS]
    def wait_for(s):
        side,j=(0,s) if s<4 else (1,s-8)
        csk(side,j).wait_recv()
    def body2(t,_):
        for s in dict.fromkeys(srcs[NLOC:]):
            at=srcs.index(s)+1
            if at<len(PAIRS):
                @pl.when(t==at)
                def _(): wait_for(s)
        return body(t,_)
    lax.fori_loop(NLOC-1,len(PAIRS),body2,0)
    for s in dict.fromkeys(srcs[NLOC:]):
        if srcs.index(s)+1>=len(PAIRS): wait_for(s)
    info=infoC(jnp.int32(len(PAIRS)-1))
    for r in range(N): C(info,r)
    for side in (0,1):
        coff(side).wait_send()
        for j in range(4): csk(side,j).wait_send()
def call1(mesh,offsets,sketch,pattern,count):
    g,dv=mesh.shape["grp"],mesh.shape["dev"]
    V=pl.BlockSpec(memory_space=pltpu.VMEM)
    return pl.pallas_call(functools.partial(k1,g,dv,count),out_shape=jax.ShapeDtypeStruct((4,512,256),F32),
      in_specs=[V,pl.BlockSpec(memory_space=pl.ANY),pl.BlockSpec(memory_space=pltpu.SMEM)],out_specs=V,
      scratch_shapes=[pltpu.VMEM((2,4,3,512),F32),pltpu.VMEM((12,512,256),BF),
        pltpu.VMEM((32,512),F32),pltpu.VMEM((4,32,512),BF),pltpu.VMEM((12,3,512),F32),pltpu.VMEM((32,512),F32),
        pltpu.VMEM((512,512),F32),pltpu.VMEM((512,512),BF),
        pltpu.SemaphoreType.DMA((2,)),pltpu.SemaphoreType.DMA((2,)),pltpu.SemaphoreType.DMA((2,4)),pltpu.SemaphoreType.DMA((2,4)),pltpu.SemaphoreType.DMA],
      compiler_params=pltpu.CompilerParams(vmem_limit_bytes=50<<20,collective_id=0,has_side_effects=True))(offsets,sketch,pattern)
def cat3(xh,xl): pass
def hl(x):
    h=x.astype(BF); return h,(x-h.astype(F32)).astype(BF)
def dot(a,b,ca=1,cb=0):
    return lax.dot_general(a,b,(((ca,),(cb,)),((),())),preferred_element_type=F32)
NB=64; R=256; NC=4
def lanes(x,j):
    return jnp.take_along_axis(x,jnp.full((8,128),j,jnp.int32),axis=1,mode="promise_in_bounds")
def rows8(x,j):
    return jnp.broadcast_to(x[j:j+1,:],(8,128))
def k2(s_ref, ord_ref, basis_ref, fac_ref, aug, xh, xl, xs):
    lane=lax.broadcasted_iota(jnp.int32,(NB,128),1)
    row=lax.broadcasted_iota(jnp.int32,(NB,128),0)
    r2=lax.broadcasted_iota(jnp.int32,(R,R),0); c2=lax.broadcasted_iota(jnp.int32,(R,R),1)
    eye=r2==c2
    for c in range(NC):
        st=s_ref[c].T
        aug[c,:,R:]=st
        th,tl=hl(st)
        g=dot(th,th,1,1)+(dot(th,tl,1,1)+dot(tl,th,1,1))
        tr=jnp.sum(jnp.where(eye,g,0.0),keepdims=True)
        shift=tr*(0.01/R)+1e-5
        aug[c,:,:R]=g+jnp.where(eye,shift,0.0)
    sub8=lax.broadcasted_iota(jnp.int32,(8,128),0)
    for jb in range(4):
        lt,half=jb//2,jb%2
        r0=jb*NB; rs=slice(r0,r0+NB); t0=lt*128; tile=slice(t0,t0+128)
        K=r0
        inA=(lane>=64) if half else (lane<64)
        other=(lane==row) if half else (lane==row+64)
        Ms=[]; lh=[None]*NC; ll=[None]*NC
        for c in range(NC):
            D=aug[c,rs,tile]
            if jb:
                lh[c]=xh[c,0:K,tile].T[64*half:64*half+64]
                ll[c]=xl[c,0:K,tile].T[64*half:64*half+64]
                bh,bl=xh[c,0:K,tile],xl[c,0:K,tile]
                D=D-(dot(lh[c],bh)+(dot(lh[c],bl)+dot(ll[c],bh)))
                aug[c,rs,tile]=D
            Mx=jnp.where(inA,D,jnp.where(other,1.0,0.0))
            Ms.append([Mx[8*g:8*g+8] for g in range(8)])
        rest=slice(t0+128,768)
        if jb:
            for c in range(NC):
                bh,bl=xh[c,0:K,rest],xl[c,0:K,rest]
                aug[c,rs,rest]=aug[c,rs,rest]-(dot(lh[c],bh)+(dot(lh[c],bl)+dot(ll[c],bh)))
        for p in range(8):
            cb=[[None]*8 for _ in range(NC)]; col=[None]*NC; v=[None]*NC
            for g in range(p,8):
                for jj in range(8):
                    for c in range(NC):
                        b=lanes(Ms[c][g],64*half+8*p+jj)
                        if g==p: cb[c][jj]={}
                        cb[c][jj][g]=b
            for c in range(NC):
                col[c]=[cb[c][jj][p] for jj in range(8)]; v[c]=Ms[c][p]
            for jj in range(8):
                isj=sub8==jj
                for c in range(NC):
                    s=lax.rsqrt(rows8(col[c][jj],jj)); s2=s*s
                    rw=rows8(v[c],jj)
                    xs[c,8*p+jj:8*p+jj+1,:]=(rw*s)[0:1]
                    q=rw*s2
                    cj=col[c][jj]
                    v[c]=jnp.where(isj,q,v[c]-cj*q)
                    for kk in range(jj+1,8):
                        qk=rows8(col[c][kk],jj)*s2
                        col[c][kk]=jnp.where(isj,qk,col[c][kk]-cj*qk)
            for c in range(NC):
                w=[rows8(v[c],jj) for jj in range(8)]
                for g in range(p+1,8):
                    t=[cb[c][jj][g]*w[jj] for jj in range(8)]
                    while len(t)>1: t=[t[i]+t[i+1] for i in range(0,len(t),2)]
                    Ms[c][g]=Ms[c][g]-t[0]
        for c in range(NC):
            X=xs[c]
            U=jnp.where(inA&((lane-64*half)>=row),X,0.0)
            Li=X[:, 0:64] if half else X[:, 64:128]
            Lh,Ll=hl(Li)
            cols=slice(t0 if half==0 else t0+128,768)
            rh,rl=hl(aug[c,rs,cols])
            P=dot(Lh,rh)+(dot(Lh,rl)+dot(Ll,rh))
            ph,pl_=hl(P)
            xh[c,rs,cols]=ph; xl[c,rs,cols]=pl_
            if half==0:
                fac_ref[c,rs,tile]=jnp.where(inA,U,P[:,0:128])
                if lt==0: fac_ref[c,rs,128:256]=P[:,128:256]
            else:
                fac_ref[c,rs,tile]=U
                if lt==0: fac_ref[c,rs,128:256]=P[:,0:128]
            if lt==1: fac_ref[c,rs,0:128]=jnp.zeros((NB,128),F32)
    of=ord_ref[...].astype(F32)
    oT=jnp.concatenate([of,of],axis=0).T
    lane5=lax.broadcasted_iota(jnp.int32,(512,512),1).astype(F32)
    for c in range(NC):
        P=jnp.where(oT[:,c:c+1]==lane5,1.0,0.0).astype(BF)
        basis_ref[c]=dot(P,xh[c,:,R:],1,1).astype(BF)
def call2(samples,order,interpret=False):
    return pl.pallas_call(k2,out_shape=[jax.ShapeDtypeStruct((4,512,256),BF),jax.ShapeDtypeStruct((4,256,256),F32)],
      in_specs=[pl.BlockSpec(memory_space=pltpu.VMEM)]*2,out_specs=[pl.BlockSpec(memory_space=pltpu.VMEM)]*2,
      scratch_shapes=[pltpu.VMEM((4,256,768),F32),pltpu.VMEM((4,256,768),BF),pltpu.VMEM((4,256,768),BF),pltpu.VMEM((4,64,128),F32)],
      compiler_params=pltpu.CompilerParams(vmem_limit_bytes=50<<20))(samples,order)
def solution(mesh):
    placed=(P(("grp","dev"),None,None),P(("grp","dev"),None,None),P(("grp","dev"),None),P(("grp","dev"),None))
    devices=mesh.shape["grp"]*mesh.shape["dev"]
    def body(offsets,sketch,pattern,point_order):
        samples=call1(mesh,offsets,sketch,pattern,offsets.shape[0]*devices)
        return tuple(call2(samples,point_order))
    return jax.shard_map(body,mesh=mesh,in_specs=placed,out_specs=(P(("grp","dev"),None,None),P(("grp","dev"),None,None)),check_vma=False)
```

```python
import math, functools
import numpy as np
import jax, jax.numpy as jnp
from jax import lax
from jax.experimental import pallas as pl
from jax.experimental.pallas import tpu as pltpu
F32=jnp.float32; BF=jnp.bfloat16
M=512
def cos_coeffs(deg):
    n=4000
    t=np.cos((np.arange(n)+.5)*np.pi/n)
    z=0.125+0.125*t
    f=np.sqrt(z)
    c=np.polynomial.chebyshev.Chebyshev.fit(z,np.cos(2*np.pi*f),deg,domain=[0,0.25])
    p=c.convert(kind=np.polynomial.Polynomial,domain=[-1,1],window=[-1,1]).coef
    return [float(v) for v in p]
def sin_coeffs(deg):
    n=4000
    t=np.cos((np.arange(n)+.5)*np.pi/n)
    z=1/32+1/32*t
    g=np.sqrt(z)
    y=-np.sin(2*np.pi*g)/g
    w=np.sqrt(g)
    V=np.vander(z*16,deg+1,increasing=True)
    for _ in range(40):
        c=np.linalg.lstsq(V*(w*g)[:,None],y*w*g,rcond=None)[0]
        e=np.abs((V@c-y)*g)
        w=w*np.sqrt(1e-3+e/e.max()); w=w/w.max()
    return [float(v*16.0**n) for n,v in enumerate(c)]
SIN=sin_coeffs(3)
SIGMA=40.0/(2*math.pi)
SCALE=1.0/math.sqrt(512)
def value(u):
    y=u*lax.rsqrt(u)
    g=jnp.abs(y-jnp.round(y))-0.25
    z=g*g
    a=SCALE*SIGMA
    p=SIN[-1]*a
    for c in SIN[-2::-1]:
        p=p*z+c*a
    h=jnp.exp2(y*(-0.25*math.log2(math.e)/SIGMA)-jnp.log2(y+0.5*SIGMA))
    return (p*g)*h
def split3(x):
    h=x.astype(BF).astype(F32); m=(x-h).astype(BF).astype(F32); return h,m,x-h-m
def prep(off, c, t_ref, s_ref):
    x=jnp.concatenate([(off[0:1]+c)-c,off[1:3]],axis=0)
    if t_ref is not None:
        a=x*SIGMA
        n=a[0:1]*a[0:1]+a[1:2]*a[1:2]+a[2:3]*a[2:3]
        h,m,l=split3(a)
        for d in range(3):
            for q,w in enumerate((h,h,m,m,h,l)): t_ref[6*d+q:6*d+q+1,:]=w[d:d+1]
        one=jnp.ones_like(n)
        for q,w in enumerate(split3(n)):
            t_ref[18+q:19+q,:]=w; t_ref[21+q:22+q,:]=one
        t_ref[24:32,:]=jnp.zeros((8,x.shape[1]),F32)
    s_ref[0:3,:]=x
def s_rows(x, o, s_ref):
    b=jnp.concatenate([x[0:1]+o,x[1:3]],axis=0)*SIGMA
    n=b[0:1]*b[0:1]+b[1:2]*b[1:2]+b[2:3]*b[2:3]
    h,m,l=[-2.0*w for w in split3(b)]
    for d in range(3):
        for q,w in enumerate((h,m,h,m,l,h)): s_ref[6*d+q:6*d+q+1,:]=w[d:d+1]
    one=jnp.ones_like(n)
    for q,w in enumerate(split3(n)):
        s_ref[18+q:19+q,:]=one; s_ref[21+q:22+q,:]=w
    s_ref[24:32,:]=jnp.zeros((8,x.shape[1]),F32)
from jax.sharding import PartitionSpec as P
MESH_ID=pl.DeviceIdType.MESH
CHR=128
L_ORDER=(2,3,1,0); R_ORDER=(1,0,2,3)
def pair_list():
    order=[4,5,6,7]
    for a,b in zip(L_ORDER,R_ORDER): order+=[a,8+b]
    return [(s,i) for s in order for i in range(4) if 2<=abs(s-4-i)<=4]
PAIRS=pair_list()
def lookup(t,table):
    v=jnp.int32(table[0])
    for n in range(1,len(table)):
        if table[n]!=table[n-1]: v=jnp.where(t>=n,table[n],v)
    return v
def dot(a,b,ca=1,cb=0):
    return lax.dot_general(a,b,(((ca,),(cb,)),((),())),preferred_element_type=F32)
def stages(sk, tp, sp, sr, pat_ref, out_ref, u_ref, k_ref, first, count, CHR):
    def decode(t):
        t=jnp.clip(t,0,len(PAIRS)-1)
        return lookup(t,[p[0] for p in PAIRS]),lookup(t,[p[1] for p in PAIRS])
    def loadA(t):
        s,i=decode(t)
        o=(s-4-i).astype(F32)
        s_rows(sp[s],o,sr)
        return tp[i],sr[...].astype(BF)
    def Aval(ops,r):
        T,S=ops
        return dot(T[:,r*CHR:(r+1)*CHR],S,0,0)
    def A(ops,r):
        T,S=ops
        u_ref[r*CHR:(r+1)*CHR,:]=dot(T[:,r*CHR:(r+1)*CHR],S,0,0)
    def B(r,k_ref=k_ref):
        k_ref[r*CHR:(r+1)*CHR,:]=value(u_ref[r*CHR:(r+1)*CHR,:]).astype(BF)
    def infoC(t):
        s,i=decode(t)
        oi=s-4-i
        k=jnp.where(oi<0,oi+4,oi+1)
        g=first+s-4
        w=jnp.where((g>=0)&(g<count)&(t>=0),pat_ref[i,k],0).astype(F32)
        return s,i,w
    def C(info,r,k_ref=k_ref):
        s,i,w=info
        rows=slice(r*CHR,(r+1)*CHR)
        out_ref[i,rows,:]=out_ref[i,rows,:]+w*dot(k_ref[rows,:],sk[s])
    return loadA,A,B,infoC,C
def k1(groups, devs, count, off_ref, sk_ref, pat_ref, ord_ref, out_ref, perm_ref, off, hoff, sk, pat, order, tf, tp, sp, sr, u_ref, k_ref, k2_ref, so, ro, ss, rsem, loc):
    d=lax.axis_index("grp")*devs+lax.axis_index("dev")
    total=groups*devs
    right=lax.rem(d+1,total); left=lax.rem(d+total-1,total)
    rid=(right//devs,lax.rem(right,devs)); lid=(left//devs,lax.rem(left,devs))
    barrier=pltpu.get_barrier_semaphore()
    for n in (lid,rid):
        pl.semaphore_signal(barrier,inc=1,device_id=n,device_id_type=MESH_ID)
    fetch=[pltpu.make_async_copy(a,b,loc.at[n]) for n,(a,b) in enumerate(((off_ref,off),(ord_ref,order),(pat_ref,pat),(sk_ref,sk.at[4:8])))]
    for f in fetch: f.start()
    first=d*4
    ff=first.astype(F32)
    def coff(side):
        return pltpu.make_async_remote_copy(off_ref,hoff.at[side],so.at[side],ro.at[side],device_id=rid if side==0 else lid,device_id_type=MESH_ID)
    def csk(side,j):
        return pltpu.make_async_remote_copy(sk_ref.at[j],sk.at[8*side+j],ss.at[side,j],rsem.at[side,j],device_id=rid if side==0 else lid,device_id_type=MESH_ID)
    pl.semaphore_wait(barrier,2)
    for side in (0,1): coff(side).start()
    for a,b in zip(L_ORDER,R_ORDER):
        csk(0,a).start(); csk(1,b).start()
    fetch[0].wait()
    for s in range(4,8):
        prep(off[:,s-4,:], ff+(s-4.0), tf, sp.at[s])
        tp[s-4]=tf[...].astype(BF)
    fetch[1].wait()
    of=order[...].astype(F32)
    oT=jnp.concatenate([of,of],axis=0).T
    lane5=lax.broadcasted_iota(jnp.int32,(M,M),1).astype(F32)
    for c in range(4):
        perm_ref[c]=jnp.where(oT[:,c:c+1]==lane5,1.0,0.0).astype(BF)
    out_ref[...]=jnp.zeros_like(out_ref)
    k_ref[...]=jnp.zeros_like(k_ref)
    fetch[2].wait()
    loadA,A,B,infoC,C=stages(sk,tp,sp,sr,pat,out_ref,u_ref,k_ref,first,count,CHR)
    N=M//CHR
    ops=loadA(jnp.int32(0))
    for r in range(N): A(ops,r)
    fetch[3].wait()
    def body(t,_):
        ops=loadA(t+1); info=infoC(t-1)
        for r in range(N):
            C(info,r); B(r); A(ops,r)
        return 0
    NLOC=6; LAST=len(PAIRS)-1
    lax.fori_loop(0,NLOC-1,body,0)
    for side in (0,1): coff(side).wait_recv()
    for s in range(4):
        prep(hoff[0,:,s,:], ff+(s-4.0), None, sp.at[s])
        prep(hoff[1,:,s,:], ff+(s+4.0), None, sp.at[8+s])
    srcs=[p[0] for p in PAIRS]
    def wait_for(s):
        side,j=(0,s) if s<4 else (1,s-8)
        csk(side,j).wait_recv()
    remote=list(dict.fromkeys(srcs[NLOC:]))
    def body2(t,_):
        for s in remote:
            at=srcs.index(s)+1
            if at<LAST:
                @pl.when(t==at)
                def _(): wait_for(s)
        return body(t,_)
    lax.fori_loop(NLOC-1,LAST,body2,0)
    for r in range(N): B(r,k2_ref)
    for s in remote:
        if srcs.index(s)+1==LAST: wait_for(s)
    info=infoC(jnp.int32(LAST-1))
    for r in range(N): C(info,r)
    for s in remote:
        if srcs.index(s)==LAST: wait_for(s)
    info=infoC(jnp.int32(LAST))
    for r in range(N): C(info,r,k2_ref)
    for side in (0,1):
        coff(side).wait_send()
        for j in range(4): csk(side,j).wait_send()
def call1(mesh,offsets,sketch,pattern,order,count):
    g,dv=mesh.shape["grp"],mesh.shape["dev"]
    V=pl.BlockSpec(memory_space=pltpu.VMEM); H=pl.BlockSpec(memory_space=pltpu.HBM)
    return pl.pallas_call(functools.partial(k1,g,dv,count),out_shape=[jax.ShapeDtypeStruct((4,512,256),F32),jax.ShapeDtypeStruct((4,512,512),BF)],
      in_specs=[H,H,H,H],out_specs=[V,V],
      scratch_shapes=[pltpu.VMEM((3,4,512),F32),pltpu.VMEM((2,3,4,512),F32),pltpu.VMEM((12,512,256),BF),
        pltpu.SMEM((4,6),jnp.int32),pltpu.VMEM((4,512),jnp.int32),
        pltpu.VMEM((32,512),F32),pltpu.VMEM((4,32,512),BF),pltpu.VMEM((12,3,512),F32),pltpu.VMEM((32,512),F32),
        pltpu.VMEM((512,512),F32),pltpu.VMEM((512,512),BF),pltpu.VMEM((512,512),BF),
        pltpu.SemaphoreType.DMA((2,)),pltpu.SemaphoreType.DMA((2,)),pltpu.SemaphoreType.DMA((2,4)),pltpu.SemaphoreType.DMA((2,4)),pltpu.SemaphoreType.DMA((4,))],
      compiler_params=pltpu.CompilerParams(vmem_limit_bytes=40<<20,collective_id=0,has_side_effects=True))(*(pltpu.with_memory_space_constraint(x,pltpu.HBM) for x in (jnp.transpose(offsets,(1,0,2)),sketch,pattern,order)))
def cat3(xh,xl): pass
def hl(x):
    h=x.astype(BF); return h,(x-h.astype(F32)).astype(BF)
def dot(a,b,ca=1,cb=0):
    return lax.dot_general(a,b,(((ca,),(cb,)),((),())),preferred_element_type=F32)
NB=64; R=256; NC=4
def lanes(x,j):
    return jnp.take_along_axis(x,jnp.full((8,128),j,jnp.int32),axis=1,mode="promise_in_bounds")
def rows8(x,j):
    return jnp.broadcast_to(x[j:j+1,:],(8,128))
def k2(s_ref, perm_ref, basis_out, fac_out, basis_ref, fac_ref, aug, xh, xl, xs, bsem, fsem):
    def fcopy(c,jb):
        rows=pl.ds(jb*NB,NB)
        return pltpu.make_async_copy(fac_ref.at[c,rows],fac_out.at[c,rows],fsem.at[c,jb])
    def bcopy(c):
        return pltpu.make_async_copy(basis_ref.at[c],basis_out.at[c],bsem.at[c])
    lane=lax.broadcasted_iota(jnp.int32,(NB,128),1)
    row=lax.broadcasted_iota(jnp.int32,(NB,128),0)
    r2=lax.broadcasted_iota(jnp.int32,(R,R),0); c2=lax.broadcasted_iota(jnp.int32,(R,R),1)
    eye=r2==c2
    for c in range(NC):
        st=s_ref[c].T
        aug[c,:,R:]=st
        th,tl=hl(st)
        g=dot(th,th,1,1)+(dot(th,tl,1,1)+dot(tl,th,1,1))
        tr=jnp.sum(jnp.where(eye,g,0.0),keepdims=True)
        shift=tr*(0.01/R)+1e-5
        aug[c,:,:R]=g+jnp.where(eye,shift,0.0)
    sub8=lax.broadcasted_iota(jnp.int32,(8,128),0)
    for jb in range(4):
        lt,half=jb//2,jb%2
        r0=jb*NB; rs=slice(r0,r0+NB); t0=lt*128; tile=slice(t0,t0+128)
        K=r0
        inA=(lane>=64) if half else (lane<64)
        other=(lane==row) if half else (lane==row+64)
        Ms=[]; lh=[None]*NC; ll=[None]*NC
        for c in range(NC):
            D=aug[c,rs,tile]
            if jb:
                lh[c]=xh[c,0:K,tile].T[64*half:64*half+64]
                ll[c]=xl[c,0:K,tile].T[64*half:64*half+64]
                bh,bl=xh[c,0:K,tile],xl[c,0:K,tile]
                D=D-(dot(lh[c],bh)+(dot(lh[c],bl)+dot(ll[c],bh)))
                aug[c,rs,tile]=D
            Mx=jnp.where(inA,D,jnp.where(other,1.0,0.0))
            Ms.append([Mx[8*g:8*g+8] for g in range(8)])
        rest=slice(t0+128,768)
        if jb:
            for c in range(NC):
                bh,bl=xh[c,0:K,rest],xl[c,0:K,rest]
                aug[c,rs,rest]=aug[c,rs,rest]-(dot(lh[c],bh)+(dot(lh[c],bl)+dot(ll[c],bh)))
        for p in range(8):
            cb=[[None]*8 for _ in range(NC)]; col=[None]*NC; v=[None]*NC
            for g in range(p,8):
                for jj in range(8):
                    for c in range(NC):
                        b=lanes(Ms[c][g],64*half+8*p+jj)
                        if g==p: cb[c][jj]={}
                        cb[c][jj][g]=b
            for c in range(NC):
                col[c]=[cb[c][jj][p] for jj in range(8)]; v[c]=Ms[c][p]
            for jj in range(8):
                isj=sub8==jj
                for c in range(NC):
                    s=lax.rsqrt(rows8(col[c][jj],jj)); s2=s*s
                    rw=rows8(v[c],jj)
                    xs[c,8*p+jj:8*p+jj+1,:]=(rw*s)[0:1]
                    q=rw*s2
                    cj=col[c][jj]
                    v[c]=jnp.where(isj,q,v[c]-cj*q)
                    for kk in range(jj+1,8):
                        qk=rows8(col[c][kk],jj)*s2
                        col[c][kk]=jnp.where(isj,qk,col[c][kk]-cj*qk)
            for c in range(NC):
                w=[rows8(v[c],jj) for jj in range(8)]
                for g in range(p+1,8):
                    t=[cb[c][jj][g]*w[jj] for jj in range(8)]
                    while len(t)>1: t=[t[i]+t[i+1] for i in range(0,len(t),2)]
                    Ms[c][g]=Ms[c][g]-t[0]
        for c in range(NC):
            X=xs[c]
            U=jnp.where(inA&((lane-64*half)>=row),X,0.0)
            Li=X[:, 0:64] if half else X[:, 64:128]
            Lh,Ll=hl(Li)
            cols=slice(t0 if half==0 else t0+128,768)
            rh,rl=hl(aug[c,rs,cols])
            P=dot(Lh,rh)+(dot(Lh,rl)+dot(Ll,rh))
            ph,pl_=hl(P)
            xh[c,rs,cols]=ph; xl[c,rs,cols]=pl_
            if half==0:
                fac_ref[c,rs,tile]=jnp.where(inA,U,P[:,0:128])
                if lt==0: fac_ref[c,rs,128:256]=P[:,128:256]
            else:
                fac_ref[c,rs,tile]=U
                if lt==0: fac_ref[c,rs,128:256]=P[:,0:128]
            if lt==1: fac_ref[c,rs,0:128]=jnp.zeros((NB,128),F32)
            fcopy(c,jb).start()
    for c in range(NC):
        basis_ref[c]=dot(perm_ref[c],xh[c,:,R:],1,1).astype(BF)
        bcopy(c).start()
    for c in range(NC):
        for jb in range(4): fcopy(c,jb).wait()
        bcopy(c).wait()
def call2(samples,perm):
    V=pl.BlockSpec(memory_space=pltpu.VMEM); H=pl.BlockSpec(memory_space=pltpu.HBM)
    return pl.pallas_call(k2,out_shape=[jax.ShapeDtypeStruct((4,512,256),BF),jax.ShapeDtypeStruct((4,256,256),F32)],
      in_specs=[V,V],out_specs=[H,H],
      scratch_shapes=[pltpu.VMEM((4,512,256),BF),pltpu.VMEM((4,256,256),F32),pltpu.VMEM((4,256,768),F32),pltpu.VMEM((4,256,768),BF),pltpu.VMEM((4,256,768),BF),pltpu.VMEM((4,64,128),F32),
        pltpu.SemaphoreType.DMA((4,)),pltpu.SemaphoreType.DMA((4,4))],
      compiler_params=pltpu.CompilerParams(vmem_limit_bytes=40<<20))(samples,perm)
def solution(mesh):
    placed=(P(("grp","dev"),None,None),P(("grp","dev"),None,None),P(("grp","dev"),None),P(("grp","dev"),None))
    devices=mesh.shape["grp"]*mesh.shape["dev"]
    def body(offsets,sketch,pattern,point_order):
        samples,perm=call1(mesh,offsets,sketch,pattern,point_order,offsets.shape[0]*devices)
        return tuple(call2(samples,perm))
    return jax.shard_map(body,mesh=mesh,in_specs=placed,out_specs=(P(("grp","dev"),None,None),P(("grp","dev"),None,None)),check_vma=False)
```

```python
import math, functools
import numpy as np
import jax, jax.numpy as jnp
from jax import lax
from jax.experimental import pallas as pl
from jax.experimental.pallas import tpu as pltpu
F32=jnp.float32; BF=jnp.bfloat16
M=512
def cos_coeffs(deg):
    n=4000
    t=np.cos((np.arange(n)+.5)*np.pi/n)
    z=0.125+0.125*t
    f=np.sqrt(z)
    c=np.polynomial.chebyshev.Chebyshev.fit(z,np.cos(2*np.pi*f),deg,domain=[0,0.25])
    p=c.convert(kind=np.polynomial.Polynomial,domain=[-1,1],window=[-1,1]).coef
    return [float(v) for v in p]
def sin_coeffs(deg):
    n=4000
    t=np.cos((np.arange(n)+.5)*np.pi/n)
    z=1/32+1/32*t
    g=np.sqrt(z)
    y=-np.sin(2*np.pi*g)/g
    w=np.sqrt(g)
    V=np.vander(z*16,deg+1,increasing=True)
    for _ in range(40):
        c=np.linalg.lstsq(V*(w*g)[:,None],y*w*g,rcond=None)[0]
        e=np.abs((V@c-y)*g)
        w=w*np.sqrt(1e-3+e/e.max()); w=w/w.max()
    return [float(v*16.0**n) for n,v in enumerate(c)]
SIN=sin_coeffs(3)
SIGMA=40.0/(2*math.pi)
SCALE=1.0/math.sqrt(512)
def value(u):
    y=u*lax.rsqrt(u)
    g=jnp.abs(y-jnp.round(y))-0.25
    z=g*g
    a=SCALE*SIGMA
    p=SIN[-1]*a
    for c in SIN[-2::-1]:
        p=p*z+c*a
    h=jnp.exp2(y*(-0.25*math.log2(math.e)/SIGMA)-jnp.log2(y+0.5*SIGMA))
    return (p*g)*h
def split3(x):
    h=x.astype(BF).astype(F32); m=(x-h).astype(BF).astype(F32); return h,m,x-h-m
def prep(off, c, t_ref, s_ref):
    x=jnp.concatenate([(off[0:1]+c)-c,off[1:3]],axis=0)
    if t_ref is not None:
        a=x*SIGMA
        n=a[0:1]*a[0:1]+a[1:2]*a[1:2]+a[2:3]*a[2:3]
        h,m,l=split3(a)
        for d in range(3):
            for q,w in enumerate((h,h,m,m,h,l)): t_ref[6*d+q:6*d+q+1,:]=w[d:d+1]
        one=jnp.ones_like(n)
        for q,w in enumerate(split3(n)):
            t_ref[18+q:19+q,:]=w; t_ref[21+q:22+q,:]=one
        t_ref[24:32,:]=jnp.zeros((8,x.shape[1]),F32)
    s_ref[0:3,:]=x
def s_rows(x, o, s_ref):
    b=jnp.concatenate([x[0:1]+o,x[1:3]],axis=0)*SIGMA
    n=b[0:1]*b[0:1]+b[1:2]*b[1:2]+b[2:3]*b[2:3]
    h,m,l=[-2.0*w for w in split3(b)]
    for d in range(3):
        for q,w in enumerate((h,m,h,m,l,h)): s_ref[6*d+q:6*d+q+1,:]=w[d:d+1]
    one=jnp.ones_like(n)
    for q,w in enumerate(split3(n)):
        s_ref[18+q:19+q,:]=one; s_ref[21+q:22+q,:]=w
    s_ref[24:32,:]=jnp.zeros((8,x.shape[1]),F32)
from jax.sharding import PartitionSpec as P
MESH_ID=pl.DeviceIdType.MESH
CHR=128
L_ORDER=(2,3,1,0); R_ORDER=(1,0,2,3)
def pair_list():
    order=[]
    for a,b in zip(L_ORDER,R_ORDER): order+=[a,8+b]
    return LOCAL+[(s,i) for s in order for i in range(4) if 2<=abs(s-4-i)<=4]
LOCAL=[(6,0),(7,0),(7,1)]
PAIRS=pair_list()
def lookup(t,table):
    v=jnp.int32(table[0])
    for n in range(1,len(table)):
        if table[n]!=table[n-1]: v=jnp.where(t>=n,table[n],v)
    return v
def dot(a,b,ca=1,cb=0):
    return lax.dot_general(a,b,(((ca,),(cb,)),((),())),preferred_element_type=F32)
def stages(sk, tp, sp, sr, pat_ref, out_ref, u_ref, k_ref, first, count, CHR):
    def decode(t):
        t=jnp.clip(t,0,len(PAIRS)-1)
        return lookup(t,[p[0] for p in PAIRS]),lookup(t,[p[1] for p in PAIRS])
    def loadA(t):
        s,i=decode(t)
        o=(s-4-i).astype(F32)
        s_rows(sp[s],o,sr)
        return tp[i],sr[...].astype(BF)
    def Aval(ops,r):
        T,S=ops
        return dot(T[:,r*CHR:(r+1)*CHR],S,0,0)
    def A(ops,r):
        T,S=ops
        u_ref[r*CHR:(r+1)*CHR,:]=dot(T[:,r*CHR:(r+1)*CHR],S,0,0)
    def B(r,k_ref=k_ref):
        k_ref[r*CHR:(r+1)*CHR,:]=value(u_ref[r*CHR:(r+1)*CHR,:]).astype(BF)
    def infoC(t):
        s,i=decode(t)
        oi=s-4-i
        k=jnp.where(oi<0,oi+4,oi+1)
        g=first+s-4
        w=jnp.where((g>=0)&(g<count)&(t>=0),pat_ref[i,k],0).astype(F32)
        return s,i,w
    def C(info,r,k_ref=k_ref):
        s,i,w=info
        rows=slice(r*CHR,(r+1)*CHR)
        out_ref[i,rows,:]=out_ref[i,rows,:]+w*dot(k_ref[rows,:],sk[s])
    def D(t):
        s,i=decode(t)
        o=i-(s-4)
        w=jnp.where(t>=0,pat_ref[s-4,jnp.where(o<0,o+4,o+1)],0).astype(F32)
        for r in range(M//CHR):
            rows=slice(r*CHR,(r+1)*CHR)
            out_ref[s-4,rows,:]=out_ref[s-4,rows,:]+w*dot(k_ref[:,rows],sk[4+i],0,0)
    return loadA,A,B,infoC,C,D
def k1(groups, devs, count, off_ref, sk_ref, pat_ref, ord_ref, out_ref, perm_ref, mid_ref, off, hoff, sk, pat, order, tf, tp, sp, sr, u_ref, k_ref, k2_ref, so, ro, ss, rsem, loc):
    d=lax.axis_index("grp")*devs+lax.axis_index("dev")
    total=groups*devs
    right=lax.rem(d+1,total); left=lax.rem(d+total-1,total)
    rid=(right//devs,lax.rem(right,devs)); lid=(left//devs,lax.rem(left,devs))
    barrier=pltpu.get_barrier_semaphore()
    for n in (lid,rid):
        pl.semaphore_signal(barrier,inc=1,device_id=n,device_id_type=MESH_ID)
    fetch=[pltpu.make_async_copy(a,b,loc.at[n]) for n,(a,b) in enumerate(((off_ref,off),(ord_ref,order),(pat_ref,pat),(sk_ref,sk.at[4:8])))]
    for f in fetch: f.start()
    first=d*4
    ff=first.astype(F32)
    def coff(side):
        return pltpu.make_async_remote_copy(off_ref,hoff.at[side],so.at[side],ro.at[side],device_id=rid if side==0 else lid,device_id_type=MESH_ID)
    def csk(side,j):
        return pltpu.make_async_remote_copy(sk_ref.at[j],sk.at[8*side+j],ss.at[side,j],rsem.at[side,j],device_id=rid if side==0 else lid,device_id_type=MESH_ID)
    pl.semaphore_wait(barrier,2)
    for side in (0,1): coff(side).start()
    for a,b in zip(L_ORDER,R_ORDER):
        csk(0,a).start(); csk(1,b).start()
    out_ref[...]=jnp.zeros_like(out_ref)
    k_ref[...]=jnp.zeros_like(k_ref)
    fetch[0].wait()
    for s in range(4,8):
        prep(off[:,s-4,:], ff+(s-4.0), tf, sp.at[s])
        tp[s-4]=tf[...].astype(BF)
    fetch[1].wait()
    of=order[...].astype(F32)
    oT=jnp.concatenate([of,of],axis=0).T
    lane5=lax.broadcasted_iota(jnp.int32,(M,M),1).astype(F32)
    for c in range(4):
        perm_ref[c]=jnp.where(oT[:,c:c+1]==lane5,1.0,0.0).astype(BF)
    fetch[2].wait()
    loadA,A,B,infoC,C,D=stages(sk,tp,sp,sr,pat,out_ref,u_ref,k_ref,first,count,CHR)
    N=M//CHR
    ops=loadA(jnp.int32(0))
    for r in range(N): A(ops,r)
    fetch[3].wait()
    def body(t,_):
        ops=loadA(t+1); info=infoC(t-1)
        for r in range(N):
            C(info,r); B(r); A(ops,r)
        return 0
    def both(t,_):
        D(t-1)
        return body(t,_)
    NLOC=len(LOCAL); LAST=len(PAIRS)-1
    lax.fori_loop(0,NLOC-1,both,0)
    for side in (0,1): coff(side).wait_recv()
    for s in range(4):
        prep(hoff[0,:,s,:], ff+(s-4.0), None, sp.at[s])
        prep(hoff[1,:,s,:], ff+(s+4.0), None, sp.at[8+s])
    srcs=[p[0] for p in PAIRS]
    def wait_for(s):
        side,j=(0,s) if s<4 else (1,s-8)
        csk(side,j).wait_recv()
    remote=list(dict.fromkeys(srcs[NLOC:]))
    def body2(t,_):
        for s in remote:
            at=srcs.index(s)+1
            if at<LAST:
                @pl.when(t==at)
                def _(): wait_for(s)
        return body(t,_)
    lax.fori_loop(NLOC-1,NLOC+1,both,0)
    lax.fori_loop(NLOC+1,LAST,body2,0)
    for r in range(N): B(r,k2_ref)
    for c in (1,2): augment(out_ref[c],mid_ref.at[c-1])
    for s in remote:
        if srcs.index(s)+1==LAST: wait_for(s)
    info=infoC(jnp.int32(LAST-1))
    for r in range(N): C(info,r)
    for s in remote:
        if srcs.index(s)==LAST: wait_for(s)
    info=infoC(jnp.int32(LAST))
    for r in range(N): C(info,r,k2_ref)
    for side in (0,1):
        coff(side).wait_send()
        for j in range(4): csk(side,j).wait_send()
def call1(mesh,offsets,sketch,pattern,order,count):
    g,dv=mesh.shape["grp"],mesh.shape["dev"]
    V=pl.BlockSpec(memory_space=pltpu.VMEM); H=pl.BlockSpec(memory_space=pltpu.HBM)
    return pl.pallas_call(functools.partial(k1,g,dv,count),out_shape=[jax.ShapeDtypeStruct((4,512,256),F32),jax.ShapeDtypeStruct((4,512,512),BF),jax.ShapeDtypeStruct((2,256,768),F32)],
      in_specs=[H,H,H,H],out_specs=[V,V,V],
      scratch_shapes=[pltpu.VMEM((3,4,512),F32),pltpu.VMEM((2,3,4,512),F32),pltpu.VMEM((12,512,256),BF),
        pltpu.SMEM((4,6),jnp.int32),pltpu.VMEM((4,512),jnp.int32),
        pltpu.VMEM((32,512),F32),pltpu.VMEM((4,32,512),BF),pltpu.VMEM((12,3,512),F32),pltpu.VMEM((32,512),F32),
        pltpu.VMEM((512,512),F32),pltpu.VMEM((512,512),BF),pltpu.VMEM((512,512),BF),
        pltpu.SemaphoreType.DMA((2,)),pltpu.SemaphoreType.DMA((2,)),pltpu.SemaphoreType.DMA((2,4)),pltpu.SemaphoreType.DMA((2,4)),pltpu.SemaphoreType.DMA((4,))],
      compiler_params=pltpu.CompilerParams(vmem_limit_bytes=40<<20,collective_id=0,has_side_effects=True))(*(pltpu.with_memory_space_constraint(x,pltpu.HBM) for x in (jnp.transpose(offsets,(1,0,2)),sketch,pattern,order)))
def cat3(xh,xl): pass
def hl(x):
    h=x.astype(BF); return h,(x-h.astype(F32)).astype(BF)
def dot(a,b,ca=1,cb=0):
    return lax.dot_general(a,b,(((ca,),(cb,)),((),())),preferred_element_type=F32)
NB=64; R=256; NC=4
def lanes(x,j):
    return jnp.take_along_axis(x,jnp.full((8,128),j,jnp.int32),axis=1,mode="promise_in_bounds")
def rows8(x,j):
    return jnp.broadcast_to(x[j:j+1,:],(8,128))
def augment(samples,ref):
    eye=lax.broadcasted_iota(jnp.int32,(R,R),0)==lax.broadcasted_iota(jnp.int32,(R,R),1)
    st=samples.T
    ref[:,R:]=st
    th,tl=hl(st)
    g=dot(th,th,1,1)+(dot(th,tl,1,1)+dot(tl,th,1,1))
    tr=jnp.sum(jnp.where(eye,g,0.0),keepdims=True)
    ref[:,:R]=g+jnp.where(eye,tr*(0.01/R)+1e-5,0.0)
def k2(s_ref, perm_ref, mid_ref, basis_out, fac_out, basis_ref, fac_ref, aug, upd, xh, xl, xs, bsem, fsem):
    def fcopy(c,jb):
        rows=pl.ds(jb*NB,NB)
        return pltpu.make_async_copy(fac_ref.at[c,rows],fac_out.at[c,rows],fsem.at[c,jb])
    def bcopy(c):
        return pltpu.make_async_copy(basis_ref.at[c],basis_out.at[c],bsem.at[c])
    lane=lax.broadcasted_iota(jnp.int32,(NB,128),1)
    row=lax.broadcasted_iota(jnp.int32,(NB,128),0)
    src=[aug.at[0],mid_ref.at[0],mid_ref.at[1],aug.at[1]]
    for c in (0,3): augment(s_ref[c],src[c])
    sub8=lax.broadcasted_iota(jnp.int32,(8,128),0)
    for jb in range(4):
        lt,half=jb//2,jb%2
        r0=jb*NB; rs=slice(r0,r0+NB); t0=lt*128; tile=slice(t0,t0+128)
        K=r0
        inA=(lane>=64) if half else (lane<64)
        other=(lane==row) if half else (lane==row+64)
        Ms=[]; lh=[None]*NC; ll=[None]*NC
        for c in range(NC):
            D=src[c][rs,tile]
            if jb:
                lh[c]=xh[c,0:K,tile].T[64*half:64*half+64]
                ll[c]=xl[c,0:K,tile].T[64*half:64*half+64]
                bh,bl=xh[c,0:K,tile],xl[c,0:K,tile]
                D=D-(dot(lh[c],bh)+(dot(lh[c],bl)+dot(ll[c],bh)))
                upd[c,:,tile]=D
            Mx=jnp.where(inA,D,jnp.where(other,1.0,0.0))
            Ms.append([Mx[8*g:8*g+8] for g in range(8)])
        rest=slice(t0+128,768)
        if jb:
            for c in range(NC):
                bh,bl=xh[c,0:K,rest],xl[c,0:K,rest]
                upd[c,:,rest]=src[c][rs,rest]-(dot(lh[c],bh)+(dot(lh[c],bl)+dot(ll[c],bh)))
        for p in range(8):
            cb=[[None]*8 for _ in range(NC)]; col=[None]*NC; v=[None]*NC
            for g in range(p,8):
                for jj in range(8):
                    for c in range(NC):
                        b=lanes(Ms[c][g],64*half+8*p+jj)
                        if g==p: cb[c][jj]={}
                        cb[c][jj][g]=b
            for c in range(NC):
                col[c]=[cb[c][jj][p] for jj in range(8)]; v[c]=Ms[c][p]
            for jj in range(8):
                isj=sub8==jj
                for c in range(NC):
                    s=lax.rsqrt(rows8(col[c][jj],jj)); s2=s*s
                    rw=rows8(v[c],jj)
                    xs[c,8*p+jj:8*p+jj+1,:]=(rw*s)[0:1]
                    q=rw*s2
                    cj=col[c][jj]
                    v[c]=jnp.where(isj,q,v[c]-cj*q)
                    for kk in range(jj+1,8):
                        qk=rows8(col[c][kk],jj)*s2
                        col[c][kk]=jnp.where(isj,qk,col[c][kk]-cj*qk)
            for c in range(NC):
                w=[rows8(v[c],jj) for jj in range(8)]
                for g in range(p+1,8):
                    t=[cb[c][jj][g]*w[jj] for jj in range(8)]
                    while len(t)>1: t=[t[i]+t[i+1] for i in range(0,len(t),2)]
                    Ms[c][g]=Ms[c][g]-t[0]
        for c in range(NC):
            X=xs[c]
            U=jnp.where(inA&((lane-64*half)>=row),X,0.0)
            Li=X[:, 0:64] if half else X[:, 64:128]
            Lh,Ll=hl(Li)
            cols=slice(t0 if half==0 else t0+128,768)
            rh,rl=hl(upd[c,:,cols] if jb else src[c][rs,cols])
            P=dot(Lh,rh)+(dot(Lh,rl)+dot(Ll,rh))
            ph,pl_=hl(P)
            xh[c,rs,cols]=ph; xl[c,rs,cols]=pl_
            if half==0:
                fac_ref[c,rs,tile]=jnp.where(inA,U,P[:,0:128])
                if lt==0: fac_ref[c,rs,128:256]=P[:,128:256]
            else:
                fac_ref[c,rs,tile]=U
                if lt==0: fac_ref[c,rs,128:256]=P[:,0:128]
            if lt==1: fac_ref[c,rs,0:128]=jnp.zeros((NB,128),F32)
            fcopy(c,jb).start()
    for c in range(NC):
        basis_ref[c]=dot(perm_ref[c],xh[c,:,R:],1,1).astype(BF)
        bcopy(c).start()
    for c in range(NC):
        for jb in range(4): fcopy(c,jb).wait()
        bcopy(c).wait()
def call2(samples,perm,mid):
    V=pl.BlockSpec(memory_space=pltpu.VMEM); H=pl.BlockSpec(memory_space=pltpu.HBM)
    return pl.pallas_call(k2,out_shape=[jax.ShapeDtypeStruct((4,512,256),BF),jax.ShapeDtypeStruct((4,256,256),F32)],
      in_specs=[V,V,V],out_specs=[H,H],
      scratch_shapes=[pltpu.VMEM((4,512,256),BF),pltpu.VMEM((4,256,256),F32),pltpu.VMEM((2,256,768),F32),pltpu.VMEM((4,64,768),F32),pltpu.VMEM((4,256,768),BF),pltpu.VMEM((4,256,768),BF),pltpu.VMEM((4,64,128),F32),
        pltpu.SemaphoreType.DMA((4,)),pltpu.SemaphoreType.DMA((4,4))],
      compiler_params=pltpu.CompilerParams(vmem_limit_bytes=40<<20))(samples,perm,mid)
def solution(mesh):
    placed=(P(("grp","dev"),None,None),P(("grp","dev"),None,None),P(("grp","dev"),None),P(("grp","dev"),None))
    devices=mesh.shape["grp"]*mesh.shape["dev"]
    def body(offsets,sketch,pattern,point_order):
        samples,perm,mid=call1(mesh,offsets,sketch,pattern,point_order,offsets.shape[0]*devices)
        return tuple(call2(samples,perm,mid))
    return jax.shard_map(body,mesh=mesh,in_specs=placed,out_specs=(P(("grp","dev"),None,None),P(("grp","dev"),None,None)),check_vma=False)
```
